32 devices in a mesh: section: 2 (over x), fsdp: 4 (over y, core), rep: 4 (over z).
Axes of the slice: x: 2, y: 2, z: 4, core: 2. Of those that a mesh axis runs over, the one named last changes fastest.
Arguments:
- inputs: float32 [32, 512, 1536], P(('fsdp', 'rep')), may hold values from -6 to 6
- cotangent: float32 [32, 512, 1536], P(('fsdp', 'rep')), may hold values from -6 to 6
- doc_ids: int32 [32, 512], P(('fsdp', 'rep')), may hold values from 0 to 3, never falling along the last dimension, each value on 1 to 256 neighbouring positions
- in_weight: bfloat16 [2, 1536, 6448], P('section', 'fsdp'), may hold values from -0.15625 to 0.15625
- out_weight: bfloat16 [2, 3072, 1536], P('section', 'fsdp'), may hold values from -0.109375 to 0.109375
- conv_weight: bfloat16 [2, 3328, 4], P('section', 'fsdp'), may hold values from -3 to 3
- conv_bias: bfloat16 [2, 3328], P('section', 'fsdp'), may hold values from -0.5 to 0.5
- step_bias: bfloat16 [2, 48], P('section', 'fsdp'), may hold values from -6.875 to -2.296875
- decay_log: bfloat16 [2, 48], P('section', 'fsdp'), may hold values from 0 to 2.765625
- skip_gain: bfloat16 [2, 48], P('section', 'fsdp'), may hold values from 0.5 to 1.5
- pre_gain: bfloat16 [2, 1536], P('section', 'fsdp'), may hold values from 0.5 to 1.5
- mix_gain: bfloat16 [2, 3072], P('section', 'fsdp'), may hold values from 0.5 to 1.5
Outputs:
- section_out: float32 [2, 32, 512, 1536], P('section', ('fsdp', 'rep'))
- section_in_grad: float32 [2, 32, 512, 1536], P('section', ('fsdp', 'rep'))
- grad_in_weight: float32 [2, 1536, 6448], P('section', 'fsdp')
- grad_out_weight: float32 [2, 3072, 1536], P('section', 'fsdp')
- grad_conv_weight: float32 [2, 3328, 4], P('section', 'fsdp')
- grad_conv_bias: float32 [2, 3328], P('section', 'fsdp')
- grad_step_bias: float32 [2, 48], P('section', 'fsdp')
- grad_decay_log: float32 [2, 48], P('section', 'fsdp')
- grad_skip_gain: float32 [2, 48], P('section', 'fsdp')
- grad_pre_gain: float32 [2, 1536], P('section', 'fsdp')
- grad_mix_gain: float32 [2, 3072], P('section', 'fsdp')
The draws below stay inside these ranges and needn't reach their ends.
Inputs may be any that keep to these rules, and one draw needn't show every extreme that they name: Along each sequence doc_ids never fall; each run of equal numbers is one document of 1 to 256 tokens, at most 4 documents a sequence, and some document has exactly 256.
All inputs are finite; a program needn't handle non-finite values.
Results may differ from the reference program's by a relative error of at most 0.017.
Values may be sent and summed in bfloat16 or wider, within the bound.
No kernel may reach another device: no remote copies, remote signals or barrier semaphores. Data moves between devices by JAX's collectives and lax.ppermute only.
A program may use at most 832 MiB of HBM per device.

```python
import math
import jax
import jax.numpy as jnp
import numpy as np
from jax import lax

D = 1536
HEADS = 48
CONV = 4
BLOCK = 256
SEQ_LEN = 512
INNER = 3072
CONVCH = 3328
NPROJ = 6448
SECTIONS = 2
SEQS = 32
N_SECTION = 2


def levels(key, extent, shards, least, largest):
    level, own = 1.0, jax.random.fold_in(key, 6)
    for dim, shards_of in shards:
        draws = jnp.exp(jax.random.uniform(jax.random.fold_in(own, dim), (shards_of,), jnp.float32, least / len(shards), largest / len(shards)))
        level = level * jnp.repeat(draws, extent[dim] // shards_of).reshape([-1 if axis == dim else 1 for axis in range(len(extent))])
    return level


def split_up(number_of, total, bound, lean):
    portions = [(1 << 20) // math.isqrt(rank ** lean) + 1 for rank in range(2, number_of + 1)]
    rest, given = total - bound - (number_of - 1), [1] * (number_of - 1)
    while rest > 0:
        candidates = [i for i in range(number_of - 1) if given[i] < bound]
        pool, budget = sum([portions[i] for i in candidates]), rest
        for i in candidates:
            addition = min(bound - given[i], max(1, budget * portions[i] // pool), rest)
            given[i] = given[i] + addition
            rest = rest - addition
    return np.array([bound] + given)


def uneven_parts(key, count, total, most, skew):
    if count == 2:
        one = jax.random.randint(key, (), max(1, total - most), min(most, total - 1) + 1)
        return jnp.stack([one, total - one])
    sizes = jnp.asarray(split_up(count, total, most, skew), jnp.int32)
    pairs = (count - 1) // 2
    giver, taker = sizes[1:1 + 2 * pairs:2], sizes[2:2 + 2 * pairs:2]
    slack = jnp.minimum(giver - 1, most - taker)
    moved = jax.random.randint(jax.random.fold_in(key, 1), (pairs,), 0, 1 << 20) % (slack + 1)
    sizes = sizes.at[1:1 + 2 * pairs:2].set(giver - moved).at[2:2 + 2 * pairs:2].set(taker + moved)
    return sizes[jax.random.permutation(jax.random.fold_in(key, 2), count)]


def scatter_about(key, shape, deviation, bound, pieces=(), kind=jnp.bfloat16):
    values = jax.random.normal(key, shape, jnp.float32) * deviation
    if len(pieces) > 0:
        values = levels(key, shape, pieces, -0.22, 0.18) * values
    return jnp.clip(values, min=-bound, max=bound).astype(kind)


def setup_inputs(seed: int = 0) -> dict:
    key_list = jax.random.split(jax.random.key(seed), 13)
    return {
        "inputs": scatter_about(key_list[0], (SEQS, SEQ_LEN, D), 1.0, 6.0, ((0, 16),), jnp.float32),
        "cotangent": scatter_about(key_list[1], (SEQS, SEQ_LEN, D), 1.0, 6.0, ((0, 16),), jnp.float32),
        "doc_ids": jax.vmap(lambda own: jnp.searchsorted(jnp.cumsum(uneven_parts(own, 4, SEQ_LEN, SEQ_LEN // 2, 0)), jnp.arange(SEQ_LEN), side="right"))(jax.random.split(key_list[2], SEQS)).reshape((SEQS, SEQ_LEN)).astype(jnp.int32),
        "in_weight": scatter_about(key_list[3], (SECTIONS, D, NPROJ), D ** -0.5, 0.15625, ((0, 2), (1, 4))),
        "out_weight": scatter_about(key_list[4], (SECTIONS, INNER, D), INNER ** -0.5, 0.109375, ((0, 2), (1, 4))),
        "conv_weight": scatter_about(key_list[5], (SECTIONS, CONVCH, CONV), CONV ** -0.5, 3.0, ((0, 2), (1, 4))),
        "conv_bias": jnp.clip(jax.random.uniform(key_list[6], (SECTIONS, CONVCH), jnp.float32, -0.5, 0.5) * levels(key_list[6], (SECTIONS, CONVCH), ((0, 2), (1, 4)), -0.4, 0.0), -0.5, 0.5).astype(jnp.bfloat16),
        "step_bias": jnp.clip(-6.875 + 4.578125 * jax.random.uniform(key_list[7], (SECTIONS, HEADS), jnp.float32) ** levels(key_list[7], (SECTIONS, HEADS), ((0, 2), (1, 4)), -0.2, 0.2), -6.875, -2.296875).astype(jnp.bfloat16),
        "decay_log": jnp.clip(2.765625 * jax.random.uniform(key_list[8], (SECTIONS, HEADS), jnp.float32) ** levels(key_list[8], (SECTIONS, HEADS), ((0, 2), (1, 4)), -0.2, 0.2), 0.0, 2.765625).astype(jnp.bfloat16),
        "skip_gain": jnp.clip(0.5 + 1.0 * jax.random.uniform(key_list[9], (SECTIONS, HEADS), jnp.float32) ** levels(key_list[9], (SECTIONS, HEADS), ((0, 2), (1, 4)), -0.2, 0.2), 0.5, 1.5).astype(jnp.bfloat16),
        "pre_gain": jnp.clip(1.0 + 0.1 * jax.random.normal(key_list[10], (SECTIONS, D), jnp.float32), 0.5, 1.5).astype(jnp.bfloat16),
        "mix_gain": jnp.clip(1.0 + 0.1 * jax.random.normal(key_list[11], (SECTIONS, INNER), jnp.float32), 0.5, 1.5).astype(jnp.bfloat16),
    }


HIGHEST = lax.Precision.HIGHEST
EPS = 1e-05
PARAM_NAMES = ('in_weight', 'out_weight', 'conv_weight', 'conv_bias', 'step_bias', 'decay_log', 'skip_gain', 'pre_gain', 'mix_gain')

@jax.custom_vjp
def low(v):
    return lax.optimization_barrier(v.astype(jnp.bfloat16)).astype(jnp.float32)

@jax.custom_vjp
def low_back(v):
    return v

def low_keep(v):
    return (low(v), None)

def low_pass(kept, grad):
    return (grad,)

def back_keep(v):
    return (v, None)

def back_low(kept, grad):
    return (low(grad),)
low.defvjp(low_keep, low_pass)
low_back.defvjp(back_keep, back_low)

def prenorm(hidden, gain):
    return hidden * lax.rsqrt(lax.optimization_barrier(jnp.mean(hidden * hidden, -1, keepdims=True)) + EPS) * gain

def block_scan(scaled, input_map, output_map, log_decay, doc_ids):
    length, head_count, head_width = scaled.shape
    block_count = length // BLOCK
    values = scaled.reshape(block_count, BLOCK, head_count, head_width)
    in_rows = input_map.reshape(block_count, BLOCK, -1)
    out_rows = output_map.reshape(block_count, BLOCK, -1)
    totals = jnp.swapaxes(jnp.cumsum(log_decay.reshape(block_count, BLOCK, head_count), axis=1), 1, 2)
    doc_blocks = doc_ids.reshape(block_count, BLOCK)
    later_pos = lax.broadcasted_iota(jnp.int32, (BLOCK, BLOCK), 0)
    earlier_pos = lax.broadcasted_iota(jnp.int32, (BLOCK, BLOCK), 1)
    same_doc = (doc_blocks[:, :, None] == doc_blocks[:, None, :]) & (earlier_pos <= later_pos)
    span_logs = totals[:, :, :, None] - totals[:, :, None, :]
    decays = jnp.exp(jnp.where(same_doc[:, None], span_logs, -jnp.inf))
    scores = jnp.einsum('btn,bsn->bts', out_rows, in_rows, precision=HIGHEST)
    inner_part = jnp.einsum('bhts,bshp->bthp', decays * scores[:, None], values, precision=HIGHEST)
    end_logs = totals[:, :, -1:]
    to_end = jnp.exp(end_logs - totals) * (doc_blocks == doc_blocks[:, -1:]).astype(jnp.float32)[:, None, :]
    states = jnp.einsum('bsn,bhs,bshp->bhnp', in_rows, to_end, values, precision=HIGHEST)
    entering = [jnp.zeros_like(states[0])]
    running = states[0]
    for block_index in range(1, block_count):
        entering.append(running)
        linked = (doc_blocks[block_index, -1] == doc_blocks[block_index - 1, -1]).astype(jnp.float32)
        running = states[block_index] + jnp.exp(end_logs[block_index])[:, :, None] * linked * running
    entered = jnp.stack(entering)
    previous_end = jnp.concatenate([doc_blocks[:1, -1:], doc_blocks[:-1, -1:]], 0)
    from_start = jnp.exp(totals) * (doc_blocks == previous_end).astype(jnp.float32)[:, None, :]
    outer_part = jnp.einsum('btn,bht,bhnp->bthp', out_rows, from_start, entered, precision=HIGHEST)
    return (inner_part + outer_part).reshape(length, head_count, head_width)

def mixer(projected, doc_ids, conv_weight, conv_bias, step_bias, decay_log, skip_gain, mix_gain):
    length = projected.shape[0]
    inner_width = mix_gain.shape[0]
    channels = conv_weight.shape[0]
    tap_count = conv_weight.shape[1]
    state_width = (channels - inner_width) // 2
    head_count = decay_log.shape[0]
    gate_part = projected[:, :inner_width]
    conv_in = projected[:, inner_width:inner_width + channels]
    step_raw = projected[:, inner_width + channels:]
    conv_out = conv_bias + conv_weight[:, tap_count - 1] * conv_in
    for offset in range(1, tap_count):
        shifted = jnp.pad(conv_in[:length - offset], ((offset, 0), (0, 0)))
        shifted_ids = jnp.pad(doc_ids[:length - offset], (offset, 0), constant_values=-1)
        same_doc = (shifted_ids == doc_ids).astype(jnp.float32)[:, None]
        conv_out = conv_out + conv_weight[:, tap_count - 1 - offset] * shifted * same_doc
    activated = jax.nn.silu(conv_out)
    values = activated[:, :inner_width].reshape(length, head_count, inner_width // head_count)
    input_map = activated[:, inner_width:inner_width + state_width]
    output_map = activated[:, inner_width + state_width:]
    step_size = jax.nn.softplus(step_raw + step_bias)
    log_decay = -jnp.exp(decay_log) * step_size
    scanned = block_scan(values * step_size[:, :, None], input_map, output_map, log_decay, doc_ids)
    gated = (scanned + skip_gain[:, None] * values).reshape(length, inner_width) * jax.nn.silu(gate_part)
    return gated * lax.rsqrt(lax.optimization_barrier(jnp.mean(gated * gated, -1, keepdims=True)) + EPS) * mix_gain

def layer(hidden, doc_ids, params):
    normed = low(prenorm(hidden, params['pre_gain']))
    projected = low_back(jnp.dot(normed, params['in_weight'], preferred_element_type=jnp.float32, precision=HIGHEST))
    mixed = low(mixer(projected, doc_ids, params['conv_weight'], params['conv_bias'], params['step_bias'], params['decay_log'], params['skip_gain'], params['mix_gain']))
    branch = low_back(jnp.dot(mixed, params['out_weight'], preferred_element_type=jnp.float32, precision=HIGHEST))
    return hidden + branch

def section_apply(hidden_all, doc_ids, params):
    seq_count = hidden_all.shape[0]
    group_size = math.gcd(seq_count, max(1, 4096 // SEQ_LEN))
    grouped = hidden_all.reshape(seq_count // group_size, group_size, SEQ_LEN, hidden_all.shape[2])
    grouped_ids = doc_ids.reshape(seq_count // group_size, group_size, SEQ_LEN)

    def one_layer(hidden, ids_row):
        return layer(hidden, ids_row, params)

    def one_group(carry, pair):
        return (carry, jax.vmap(one_layer)(pair[0], pair[1]))
    unused, outputs = lax.scan(jax.checkpoint(one_group), jnp.zeros((), jnp.float32), (grouped, grouped_ids))
    return outputs.reshape(hidden_all.shape)

def stack_grad(param_grads, param_name):
    return jnp.stack([entry[param_name] for entry in param_grads])

def reference(inputs, cotangent, doc_ids, in_weight, out_weight, conv_weight, conv_bias, step_bias, decay_log, skip_gain, pre_gain, mix_gain):
    stacked = dict(zip(PARAM_NAMES, (in_weight, out_weight, conv_weight, conv_bias, step_bias, decay_log, skip_gain, pre_gain, mix_gain)))

    def run_section(hidden_all, section_params):
        return section_apply(hidden_all, doc_ids, section_params)
    hidden = inputs
    outputs = []
    section_backs = []
    for section_index in range(N_SECTION):
        params = {param_name: param_value[section_index].astype(jnp.float32) for param_name, param_value in stacked.items()}
        result, section_back = jax.vjp(run_section, hidden, params)
        outputs.append(result)
        section_backs.append(section_back)
        hidden = low(result)
    upstream = cotangent
    in_grads = [None] * N_SECTION
    param_grads = [None] * N_SECTION
    for section_index in reversed(range(N_SECTION)):
        hidden_grad, grads_here = section_backs[section_index](upstream)
        in_grads[section_index] = hidden_grad
        param_grads[section_index] = grads_here
        upstream = low(hidden_grad)
    return (jnp.stack(outputs), jnp.stack(in_grads), stack_grad(param_grads, 'in_weight'), stack_grad(param_grads, 'out_weight'), stack_grad(param_grads, 'conv_weight'), stack_grad(param_grads, 'conv_bias'), stack_grad(param_grads, 'step_bias'), stack_grad(param_grads, 'decay_log'), stack_grad(param_grads, 'skip_gain'), stack_grad(param_grads, 'pre_gain'), stack_grad(param_grads, 'mix_gain'))
```

```python
import jax
import jax.numpy as jnp
from jax import lax
from jax.experimental import pallas as pl
from jax.experimental.pallas import tpu as pltpu
from jax.sharding import PartitionSpec as P

HIGHEST = lax.Precision.HIGHEST
EPS = 1e-05
SB = 128
REACH = 2
HG = 4
HW = 64
GW = HG * HW
LOG2E = 1.4426950408889634


def dotf(a, b, precision=None):
    return lax.dot_general(a, b, (((1,), (0,)), ((), ())), precision=precision,
                           preferred_element_type=jnp.float32)


def dot_nt(a, b, precision=None):
    return lax.dot_general(a, b, (((1,), (1,)), ((), ())), precision=precision,
                           preferred_element_type=jnp.float32)


def dot_tn(a, b, precision=None):
    return lax.dot_general(a, b, (((0,), (0,)), ((), ())), precision=precision,
                           preferred_element_type=jnp.float32)


def sigmoid(v):
    return 0.5 * jnp.tanh(0.5 * v) + 0.5


def conv(v, cp, tok):
    out = cp[4:5] + cp[3:4] * v
    for o in range(1, 4):
        out = out + cp[3 - o:4 - o] * (pltpu.roll(v, o, 0) * tok[:, o:o + 1])
    return out


def conv_back(v, dout, cp, tok):
    length = v.shape[0]
    dv = cp[3:4] * dout
    taps = [None] * 4
    taps[3] = jnp.sum(dout * v, 0, keepdims=True)
    for o in range(1, 4):
        m = dout * tok[:, o:o + 1]
        dv = dv + cp[3 - o:4 - o] * pltpu.roll(m, length - o, 0)
        taps[3 - o] = jnp.sum(m * pltpu.roll(v, o, 0), 0, keepdims=True)
    return dv, taps, jnp.sum(dout, 0, keepdims=True)


def head_spread(g, transposed):
    shape = (GW, 128) if transposed else (128, GW)
    lane = lax.broadcasted_iota(jnp.int32, shape, 0 if transposed else 1)
    head = lax.broadcasted_iota(jnp.int32, shape, 1 if transposed else 0)
    first = lane - (head - HG * g) * HW
    return ((first >= 0) & (first < HW)).astype(jnp.float32)


def softplus(v):
    return jnp.maximum(v, 0.0) + jnp.log1p(jnp.exp(-jnp.abs(v)))


def prepare(tail_ref, tok, hp_ref, step_scr, cumg_scr, cumt_scr, groups):
    length = tok.shape[0]
    row = lax.broadcasted_iota(jnp.int32, (length, 128), 0)
    raw = tail_ref[0, :, 256:384] + hp_ref[0:1, :]
    step = softplus(raw)
    total = step * hp_ref[1:2, :]
    k = 1
    while k < length:
        total = total + jnp.where(row >= k, pltpu.roll(total, k, 0), 0.0)
        k *= 2
    total = total * LOG2E
    step_scr[...] = step
    cumt_scr[...] = total.T
    for g in range(groups):
        cumg_scr[g] = pltpu.roll(total, (128 - HG * g) % 128, 1)


def pair_mask(i, j, tok, docrow, swap):
    ids = tok[(j if swap else i) * SB:((j if swap else i) + 1) * SB, 0:1]
    other = docrow[:, (i if swap else j) * SB:((i if swap else j) + 1) * SB]
    same = ids == other
    if i == j:
        r = lax.broadcasted_iota(jnp.int32, (SB, SB), 0)
        c = lax.broadcasted_iota(jnp.int32, (SB, SB), 1)
        same = same & ((c >= r) if swap else (c <= r))
    return same


def fwd_kernel(main_ref, tail_ref, tok_ref, doc_ref, cpx_ref, cpt_ref, hp_ref,
               gg_ref, ysc_ref, ss_ref, msc_scr, step_scr, cumg_scr, cumt_scr):
    g = pl.program_id(1)
    length = tok_ref.shape[1]
    blocks = length // SB
    groups = cumg_scr.shape[0]
    tok = tok_ref[0]

    @pl.when(g == 0)
    def _():
        prepare(tail_ref, tok, hp_ref, step_scr, cumg_scr, cumt_scr, groups)
        cpt = cpt_ref[...]
        bc = conv(tail_ref[0, :, :256], cpt, tok)
        bc = bc * sigmoid(bc)
        bmat, cmat = bc[:, :128], bc[:, 128:]
        docrow = doc_ref[0]
        for i in range(blocks):
            j0 = max(0, i - REACH)
            for j in range(j0, i + 1):
                sc = dot_nt(cmat[i * SB:(i + 1) * SB], bmat[j * SB:(j + 1) * SB], HIGHEST)
                msc_scr[i, :, (j - j0) * SB:(j - j0 + 1) * SB] = jnp.where(
                    pair_mask(i, j, tok, docrow, False), sc, 0.0)

    cp = cpx_ref[...]
    v = conv(main_ref[0, :, GW:], cp, tok)
    xa = v * sigmoid(v)
    stepw = dotf(step_scr[...], head_spread(g, False), HIGHEST)
    xt = (xa * stepw).astype(jnp.bfloat16)
    cumc = cumg_scr[g]
    low_half = lax.broadcasted_iota(jnp.int32, (SB, 128), 1) < HW
    for p in range(HG // 2):
        lanes = slice(p * 128, (p + 1) * 128)
        xp = xt[:, lanes]
        rows = [cumt_scr[pl.ds(HG * g + 2 * p + hh, 1), :] for hh in range(2)]
        for i in range(blocks):
            j0 = max(0, i - REACH)
            width = (i + 1 - j0) * SB
            ts = slice(i * SB, (i + 1) * SB)
            qs = slice(j0 * SB, (i + 1) * SB)
            parts = []
            for hh in range(2):
                col = cumc[ts, 2 * p + hh:2 * p + hh + 1]
                decay = jnp.exp2(jnp.minimum(col - rows[hh][:, qs], 0.0))
                w = (decay * msc_scr[i, :, :width]).astype(jnp.bfloat16)
                parts.append(dotf(w, xp[qs]))
            ysc_ref[0, ts, lanes] = jnp.where(low_half, parts[0], parts[1])
    z = main_ref[0, :, :GW]
    gated = (ysc_ref[0] + cp[6:7] * xa) * (z * sigmoid(z))
    gg_ref[0] = (gated * cp[5:6]).astype(jnp.bfloat16)
    sq = gated * gated
    sq = sq[:, :128] + sq[:, 128:]

    @pl.when(g == 0)
    def _():
        ss_ref[0] = sq

    @pl.when(g > 0)
    def _():
        ss_ref[0] = ss_ref[0] + sq


def mixer_forward(proj, tok, docrow, cp, hp):
    seqs, length, width = proj.shape
    groups = width // (2 * GW) - 1
    blocks = length // SB
    cost = pl.CostEstimate(flops=seqs * groups * HG * length * 400 * 128 * 2,
                           transcendentals=seqs * groups * HG * length * 400,
                           bytes_accessed=seqs * length * (width * 4 + groups * GW * 6))
    return pl.pallas_call(
        fwd_kernel,
        grid=(seqs, groups),
        in_specs=[
            pl.BlockSpec((1, length, 2 * GW), lambda s, g: (s, 0, g)),
            pl.BlockSpec((1, length, 2 * GW), lambda s, g: (s, 0, groups)),
            pl.BlockSpec((1, length, 8), lambda s, g: (s, 0, 0)),
            pl.BlockSpec((1, 1, length), lambda s, g: (s, 0, 0)),
            pl.BlockSpec((8, GW), lambda s, g: (0, g)),
            pl.BlockSpec((8, GW), lambda s, g: (0, groups)),
            pl.BlockSpec((8, 128), lambda s, g: (0, 0)),
        ],
        out_specs=[
            pl.BlockSpec((1, length, GW), lambda s, g: (s, 0, g)),
            pl.BlockSpec((1, length, GW), lambda s, g: (s, 0, g)),
            pl.BlockSpec((1, length, 128), lambda s, g: (s, 0, 0)),
        ],
        out_shape=[
            jax.ShapeDtypeStruct((seqs, length, groups * GW), jnp.bfloat16),
            jax.ShapeDtypeStruct((seqs, length, groups * GW), jnp.float32),
            jax.ShapeDtypeStruct((seqs, length, 128), jnp.float32),
        ],
        scratch_shapes=[
            pltpu.VMEM((blocks, SB, (REACH + 1) * SB), jnp.float32),
            pltpu.VMEM((length, 128), jnp.float32),
            pltpu.VMEM((groups, length, 128), jnp.float32),
            pltpu.VMEM((128, length), jnp.float32),
        ],
        compiler_params=pltpu.CompilerParams(
            dimension_semantics=("arbitrary", "arbitrary"), vmem_limit_bytes=48 << 20),
        cost_estimate=cost,
        name="mixer_forward",
    )(proj, proj, tok, docrow, cp, cp, hp)


def bwd_kernel(main_ref, tail_ref, ysc_ref, dm_ref, coef_ref, tok_ref, doc_ref, cpx_ref,
               cpt_ref, hp_ref, dproj_ref, col_ref, head_ref,
               msc_scr, step_scr, cumg_scr, cumt_scr, bc_scr, dsc_scr, dxt_scr, dcum_scr,
               dstep_scr):
    g = pl.program_id(1)
    length = tok_ref.shape[1]
    blocks = length // SB
    groups = cumg_scr.shape[0]
    tok = tok_ref[0]

    @pl.when(g == 0)
    def _():
        prepare(tail_ref, tok, hp_ref, step_scr, cumg_scr, cumt_scr, groups)
        cpt = cpt_ref[...]
        bc = conv(tail_ref[0, :, :256], cpt, tok)
        bc = bc * sigmoid(bc)
        bc_scr[...] = bc.astype(jnp.bfloat16)
        bmat, cmat = bc[:, :128], bc[:, 128:]
        docrow = doc_ref[0]
        for j in range(blocks):
            for i in range(j, min(blocks, j + REACH + 1)):
                sc = dot_nt(bmat[j * SB:(j + 1) * SB], cmat[i * SB:(i + 1) * SB], HIGHEST)
                msc_scr[j, :, (i - j) * SB:(i - j + 1) * SB] = jnp.where(
                    pair_mask(i, j, tok, docrow, True), sc, 0.0)
        dsc_scr[...] = jnp.zeros_like(dsc_scr)
        dcum_scr[...] = jnp.zeros_like(dcum_scr)
        dstep_scr[...] = jnp.zeros_like(dstep_scr)
        head_ref[0] = jnp.zeros_like(head_ref[0])

    @pl.when(g < groups)
    def _():
        cp = cpx_ref[...]
        vin = main_ref[0, :, GW:]
        v = conv(vin, cp, tok)
        sg = sigmoid(v)
        xa = v * sg
        dsilu_v = sg + xa * (1.0 - sg)
        z = main_ref[0, :, :GW]
        sz = sigmoid(z)
        silu_z = z * sz
        ysc = ysc_ref[0]
        y = ysc + cp[6:7] * xa
        gated = y * silu_z
        dm = dm_ref[0].astype(jnp.float32)
        col_ref[0, 5:6] = jnp.sum(dm * gated, 0, keepdims=True)
        dgated = dm * cp[5:6] - gated * coef_ref[0, :, 0:1]
        dy = dgated * silu_z
        dz = dgated * y * (sz + silu_z * (1.0 - sz))
        dproj_ref[0, :, :GW] = dz.astype(jnp.bfloat16)
        col_ref[0, 6:7] = jnp.sum(dy * xa, 0, keepdims=True)
        stepw = dotf(step_scr[...], head_spread(g, False), HIGHEST)
        xtb = (xa * stepw).astype(jnp.bfloat16)
        dyb = dy.astype(jnp.bfloat16)
        cumc = cumg_scr[g]
        low_half = lax.broadcasted_iota(jnp.int32, (SB, 128), 1) < HW
        zero = jnp.zeros((SB, 128), jnp.bfloat16)
        for p in range(HG // 2):
            lanes = slice(p * 128, (p + 1) * 128)
            dyp = dyb[:, lanes]
            rows = [cumt_scr[pl.ds(HG * g + 2 * p + hh, 1), :] for hh in range(2)]
            for j in range(blocks):
                i1 = min(blocks, j + REACH + 1)
                width = (i1 - j) * SB
                qs = slice(j * SB, (j + 1) * SB)
                ts = slice(j * SB, i1 * SB)
                xq = xtb[qs, lanes]
                parts = []
                acc = dsc_scr[j, :, :width]
                for hh in range(2):
                    col = cumc[qs, 2 * p + hh:2 * p + hh + 1]
                    decay = jnp.exp2(jnp.minimum(rows[hh][:, ts] - col, 0.0))
                    w = (decay * msc_scr[j, :, :width]).astype(jnp.bfloat16)
                    parts.append(dotf(w, dyp[ts]))
                    xm = jnp.where(low_half, xq, zero) if hh == 0 else jnp.where(low_half, zero, xq)
                    acc = acc + dot_nt(xm, dyp[ts]) * decay
                dsc_scr[j, :, :width] = acc
                dxt_scr[qs, lanes] = jnp.where(low_half, parts[0], parts[1])
        dxt = dxt_scr[...]
        gather = head_spread(g, True)
        dcum_scr[...] += dotf(dyb.astype(jnp.float32) * ysc - xtb.astype(jnp.float32) * dxt,
                              gather, HIGHEST)
        dstep_scr[...] += dotf(dxt * xa, gather, HIGHEST)
        dxa = dxt * stepw + cp[6:7] * dy
        dvin, taps, bias = conv_back(vin, dxa * dsilu_v, cp, tok)
        dproj_ref[0, :, GW:] = dvin.astype(jnp.bfloat16)
        for k in range(4):
            col_ref[0, k:k + 1] = taps[k]
        col_ref[0, 4:5] = bias
        col_ref[0, 7:8] = jnp.zeros_like(bias)

    @pl.when(g == groups)
    def _():
        cpt = cpt_ref[...]
        docrow = doc_ref[0]
        vin = tail_ref[0, :, :256]
        v = conv(vin, cpt, tok)
        sg = sigmoid(v)
        dsilu_v = sg + v * sg * (1.0 - sg)
        db = [None] * blocks
        dc = [None] * blocks
        for j in range(blocks):
            for i in range(j, min(blocks, j + REACH + 1)):
                ds = jnp.where(pair_mask(i, j, tok, docrow, True),
                               dsc_scr[j, :, (i - j) * SB:(i - j + 1) * SB], 0.0).astype(jnp.bfloat16)
                tb = dotf(ds, bc_scr[i * SB:(i + 1) * SB, 128:])
                tc = dot_tn(ds, bc_scr[j * SB:(j + 1) * SB, :128])
                db[j] = tb if db[j] is None else db[j] + tb
                dc[i] = tc if dc[i] is None else dc[i] + tc
        for i in range(blocks):
            dxt_scr[i * SB:(i + 1) * SB, :128] = db[i]
            dxt_scr[i * SB:(i + 1) * SB, 128:] = dc[i]
        dvin, taps, bias = conv_back(vin, dxt_scr[...] * dsilu_v, cpt, tok)
        dproj_ref[0, :, :256] = dvin.astype(jnp.bfloat16)
        for k in range(4):
            col_ref[0, k:k + 1] = taps[k]
        col_ref[0, 4:5] = bias
        col_ref[0, 5:8] = jnp.zeros((3, 256), jnp.float32)
        dlog = dcum_scr[...]
        ids = jnp.broadcast_to(tok[:, 0:1], (length, 128))
        row = lax.broadcasted_iota(jnp.int32, (length, 128), 0)
        k = 1
        while k < length:
            same = (pltpu.roll(ids, length - k, 0) == ids) & (row < length - k)
            dlog = dlog + jnp.where(same, pltpu.roll(dlog, length - k, 0), 0.0)
            k *= 2
        raw = tail_ref[0, :, 256:384] + hp_ref[0:1, :]
        rate = hp_ref[1:2, :]
        dstep = dstep_scr[...] + dlog * rate
        draw = dstep * jax.nn.sigmoid(raw)
        dproj_ref[0, :, 256:384] = draw.astype(jnp.bfloat16)
        dproj_ref[0, :, 384:] = jnp.zeros((length, 128), jnp.bfloat16)
        head_ref[0, 0:1] = jnp.sum(draw, 0, keepdims=True)
        head_ref[0, 1:2] = jnp.sum(dlog * rate * step_scr[...], 0, keepdims=True)


def mixer_backward(proj, ysc, dm, coef, tok, docrow, cp, hp):
    seqs, length, width = proj.shape
    groups = width // (2 * GW) - 1
    blocks = length // SB
    last = groups - 1
    cost = pl.CostEstimate(flops=seqs * groups * HG * length * 800 * 128 * 2,
                           transcendentals=seqs * groups * HG * length * 400,
                           bytes_accessed=seqs * length * (width * 6 + groups * GW * 8))
    return pl.pallas_call(
        bwd_kernel,
        grid=(seqs, groups + 1),
        in_specs=[
            pl.BlockSpec((1, length, 2 * GW), lambda s, g: (s, 0, jnp.minimum(g, last))),
            pl.BlockSpec((1, length, 2 * GW), lambda s, g: (s, 0, groups)),
            pl.BlockSpec((1, length, GW), lambda s, g: (s, 0, jnp.minimum(g, last))),
            pl.BlockSpec((1, length, GW), lambda s, g: (s, 0, jnp.minimum(g, last))),
            pl.BlockSpec((1, length, 8), lambda s, g: (s, 0, 0)),
            pl.BlockSpec((1, length, 8), lambda s, g: (s, 0, 0)),
            pl.BlockSpec((1, 1, length), lambda s, g: (s, 0, 0)),
            pl.BlockSpec((8, GW), lambda s, g: (0, jnp.minimum(g, last))),
            pl.BlockSpec((8, GW), lambda s, g: (0, groups)),
            pl.BlockSpec((8, 128), lambda s, g: (0, 0)),
        ],
        out_specs=[
            pl.BlockSpec((1, length, 2 * GW), lambda s, g: (s, 0, g)),
            pl.BlockSpec((1, 8, GW), lambda s, g: (s, 0, g)),
            pl.BlockSpec((1, 8, 128), lambda s, g: (s, 0, 0)),
        ],
        out_shape=[
            jax.ShapeDtypeStruct((seqs, length, width), jnp.bfloat16),
            jax.ShapeDtypeStruct((seqs, 8, (groups + 1) * GW), jnp.float32),
            jax.ShapeDtypeStruct((seqs, 8, 128), jnp.float32),
        ],
        scratch_shapes=[
            pltpu.VMEM((blocks, SB, (REACH + 1) * SB), jnp.float32),
            pltpu.VMEM((length, 128), jnp.float32),
            pltpu.VMEM((groups, length, 128), jnp.float32),
            pltpu.VMEM((128, length), jnp.float32),
            pltpu.VMEM((length, 256), jnp.bfloat16),
            pltpu.VMEM((blocks, SB, (REACH + 1) * SB), jnp.float32),
            pltpu.VMEM((length, GW), jnp.float32),
            pltpu.VMEM((length, 128), jnp.float32),
            pltpu.VMEM((length, 128), jnp.float32),
        ],
        compiler_params=pltpu.CompilerParams(
            dimension_semantics=("arbitrary", "arbitrary"), vmem_limit_bytes=56 << 20),
        cost_estimate=cost,
        name="mixer_backward",
    )(proj, proj, ysc, dm, coef, tok, docrow, cp, cp, hp)


def prenorm(hidden, gain):
    return hidden * lax.rsqrt(jnp.mean(hidden * hidden, -1, keepdims=True) + EPS) * gain


def prenorm_back(hidden, gain, dnorm):
    inv = lax.rsqrt(jnp.mean(hidden * hidden, -1, keepdims=True) + EPS)
    scaled = hidden * inv
    dgain = jnp.sum(dnorm * scaled, 0)
    dn = dnorm * gain
    return inv * (dn - scaled * jnp.mean(dn * scaled, -1, keepdims=True)), dgain


def head_lists(heads, shards):
    per = heads // shards
    if per % 2 == 0:
        return [[f * per + x * (per // 2) + i for f in range(shards) for i in range(per // 2)]
                for x in range(2)]
    return [list(range(x * (heads // 2), (x + 1) * (heads // 2))) for x in range(2)]


def runs(items):
    out = []
    for item in items:
        if out and out[-1][1] == item:
            out[-1][1] = item + 1
        else:
            out.append([item, item + 1])
    return out


def take(value, items, width, base, axis):
    return [lax.slice_in_dim(value, base + a * width, base + b * width, axis=axis)
            for a, b in runs(items)]


def pick(x, first, second):
    return jnp.where(x == 0, first, second)


def local_columns(weight, heads, inner, state):
    pieces = []
    for g in range(len(heads) // HG):
        mine = heads[g * HG:(g + 1) * HG]
        pieces += take(weight, mine, HW, 0, 1) + take(weight, mine, HW, inner, 1)
    pieces.append(weight[:, 2 * inner:2 * inner + 2 * state])
    pieces += take(weight, heads, 1, 2 * inner + 2 * state, 1)
    pad = 2 * GW - 2 * state - len(heads)
    pieces.append(jnp.zeros((weight.shape[0], pad), weight.dtype))
    return jnp.concatenate(pieces, 1)


def canonical_columns(parts, lists, inner, state):
    where = {h: (x, k) for x in range(2) for k, h in enumerate(lists[x])}
    heads = len(where)

    def column(h, kind):
        x, k = where[h]
        return x, (k // HG) * 2 * GW + kind * GW + (k % HG) * HW, HW

    def collect(spans):
        merged = []
        for x, start, size in spans:
            if merged and merged[-1][0] == x and merged[-1][2] == start:
                merged[-1][2] = start + size
            else:
                merged.append([x, start, start + size])
        return [parts[x][:, a:b] for x, a, b in merged]

    tail = (len(lists[0]) // HG) * 2 * GW
    pieces = collect([column(h, 0) for h in range(heads)])
    pieces += collect([column(h, 1) for h in range(heads)])
    both = slice(tail, tail + 2 * state)
    pieces.append(parts[0][:, both] + parts[1][:, both])
    pieces += collect([(where[h][0], tail + 2 * state + where[h][1], 1) for h in range(heads)])
    return jnp.concatenate(pieces, 1)


def per_device(inputs, cotangent, doc_ids, in_weight, out_weight, conv_weight, conv_bias,
               step_bias, decay_log, skip_gain, pre_gain, mix_gain):
    x = lax.axis_index("section")
    shards = lax.axis_size("fsdp")
    shard = lax.axis_index("fsdp")
    seqs, length, width = inputs.shape
    inner = mix_gain.shape[1] * shards
    heads = decay_log.shape[1] * shards
    taps = conv_weight.shape[2]
    channels = conv_bias.shape[1] * shards
    state = (channels - inner) // 2
    lists = head_lists(heads, shards)
    even = (heads // shards) % 2 == 0
    half = inner // 2
    swap = [(0, 1), (1, 0)]

    def across(value):
        return lax.ppermute(value, "section", swap)

    small = [conv_weight[0].reshape(-1), conv_bias[0], step_bias[0], decay_log[0], skip_gain[0],
             pre_gain[0], mix_gain[0]]
    sizes = [v.shape[0] for v in small]
    flat = lax.all_gather(jnp.concatenate(small), ("section", "fsdp"), axis=0)
    flat = flat.astype(jnp.float32).reshape(2, shards, -1)
    small_parts = []
    start = 0
    for size in sizes:
        small_parts.append(flat[:, :, start:start + size])
        start += size
    conv_w = small_parts[0].reshape(2, channels, taps)
    conv_b, step_b, decay, skip, pre, mix = [v.reshape(2, -1) for v in small_parts[1:]]

    def local_rows(values, fill):
        return pick(x, *[jnp.concatenate(take(values, lists[k], fill, 0, 1), 1) for k in range(2)])

    def chans(values):
        return jnp.concatenate([local_rows(values[:, :inner], HW), values[:, inner:]], 1)

    cps, hps = [], []
    taps_local = [chans(conv_w[:, :, k]) for k in range(taps)]
    bias_local = chans(conv_b)
    wide = lambda v: jnp.pad(v, ((0, 0), (0, 2 * state)))
    mix_local = wide(local_rows(mix, HW))
    skip_local = wide(jnp.repeat(local_rows(skip, 1), HW, axis=1))
    step_local = jnp.pad(local_rows(step_b, 1), ((0, 0), (0, 128 - heads // 2)))
    rate_local = jnp.pad(-jnp.exp(local_rows(decay, 1)), ((0, 0), (0, 128 - heads // 2)))
    zero_row = jnp.zeros_like(bias_local)
    cp_all = jnp.stack(taps_local + [bias_local, mix_local, skip_local, zero_row], 1)
    hp_all = jnp.stack([step_local, rate_local] + [jnp.zeros_like(rate_local)] * 6, 1)

    in_both = [local_columns(in_weight[0], lists[k], inner, state) for k in range(2)]
    in_mine, in_other = pick(x, *in_both), pick(x, *in_both[::-1])
    in_far = across(in_other)
    in_shards = [pick(x, in_mine, in_far), pick(x, in_far, in_mine)]
    in_full = [lax.all_gather(v, "fsdp", axis=0, tiled=True) for v in in_shards]
    if even:
        per = half // shards
        out_both = [out_weight[0, :per], out_weight[0, per:]]
        out_mine, out_other = pick(x, *out_both), pick(x, *out_both[::-1])
        out_far = across(out_other)
        out_full = [lax.all_gather(v, "fsdp", axis=0, tiled=True)
                    for v in (pick(x, out_mine, out_far), pick(x, out_far, out_mine))]
    else:
        whole = lax.all_gather(out_weight[0], "fsdp", axis=0, tiled=True)
        out_both = [whole[:half], whole[half:]]
        out_mine, out_other = pick(x, *out_both), pick(x, *out_both[::-1])
        out_far = across(out_other)
        out_full = [pick(x, out_mine, out_far), pick(x, out_far, out_mine)]

    ids = doc_ids.astype(jnp.float32)
    links = [ids]
    for o in range(1, taps):
        links.append((jnp.pad(doc_ids[:, :length - o], ((0, 0), (o, 0)), constant_values=-1)
                      == doc_ids).astype(jnp.float32))
    tok = jnp.stack(links + [jnp.zeros_like(ids)] * (8 - taps), -1)
    docrow = ids[:, None]

    saved = [[None] * seqs for _ in range(2)]
    outputs = [[None] * seqs for _ in range(2)]
    hidden = [inputs[i] for i in range(seqs)]
    for s in range(2):
        for i in range(seqs):
            h = hidden[i]
            normed = prenorm(h, pre[s]).astype(jnp.bfloat16)
            proj = dotf(normed, in_full[s])
            gg, ysc, ss = mixer_forward(proj[None], tok[i:i + 1], docrow[i:i + 1], cp_all[s],
                                        hp_all[s])
            ss = jnp.sum(ss[0], -1, keepdims=True)
            part = dotf(gg[0], out_full[s]).astype(jnp.bfloat16)
            u = part.astype(jnp.float32) + across(part).astype(jnp.float32)
            r = lax.rsqrt((ss + across(ss)) / inner + EPS)
            result = h + r * u
            outputs[s][i] = result
            saved[s][i] = (h, normed, proj, gg, ysc, u, r)
            hidden[i] = result.astype(jnp.bfloat16).astype(jnp.float32)

    grads_in, grads_out, grads_small = [None] * 2, [None] * 2, [None] * 2
    in_grads = [[None] * seqs for _ in range(2)]
    upstream = [cotangent[i] for i in range(seqs)]
    for s in (1, 0):
        din, dout, dsmall = None, None, None
        for i in range(seqs):
            h, normed, proj, gg, ysc, u, r = saved[s][i]
            g = upstream[i]
            gr = (r * g).astype(jnp.bfloat16)
            dm = dot_nt(gr, out_full[s])
            coef = r * r * jnp.sum(gr.astype(jnp.float32) * u, -1, keepdims=True) / inner
            dproj, col, head = mixer_backward(
                proj[None], ysc, dm[None], jnp.pad(coef, ((0, 0), (0, 7)))[None], tok[i:i + 1],
                docrow[i:i + 1], cp_all[s], hp_all[s])
            dnp = dot_nt(dproj[0], in_full[s]).astype(jnp.bfloat16)
            dn = dnp.astype(jnp.float32) + across(dnp).astype(jnp.float32)
            dh, dpre = prenorm_back(h, pre[s], dn)
            dh = g + dh
            in_grads[s][i] = dh
            upstream[i] = dh.astype(jnp.bfloat16).astype(jnp.float32)
            t_in, t_out = dot_tn(normed, dproj[0]), dot_tn(gg[0], gr)
            t_small = jnp.concatenate([col[0].reshape(-1), head[0, :2].reshape(-1), dpre])
            if i == 0:
                din, dout, dsmall = t_in, t_out, t_small
            else:
                din, dout, dsmall = din + t_in, dout + t_out, dsmall + t_small
        grads_in[s] = lax.psum_scatter(din.astype(jnp.bfloat16), "fsdp", scatter_dimension=0,
                                       tiled=True)
        if even:
            grads_out[s] = lax.psum_scatter(dout.astype(jnp.bfloat16), "fsdp",
                                            scatter_dimension=0, tiled=True)
        else:
            grads_out[s] = dout.astype(jnp.bfloat16)
        grads_small[s] = lax.psum(dsmall, ("fsdp", "rep"))

    def arrange(pair):
        keep, send = pick(x, *pair), pick(x, *pair[::-1])
        got = across(send)
        return [pick(x, keep, got), pick(x, got, keep)], keep

    parts, _ = arrange(grads_in)
    grad_in = lax.psum(canonical_columns(parts, lists, inner, state), "rep").astype(jnp.float32)
    parts, _ = arrange(grads_out)
    grad_out = jnp.concatenate(parts, 0)
    if not even:
        grad_out = lax.psum_scatter(grad_out, "fsdp", scatter_dimension=0, tiled=True)
    grad_out = lax.psum(grad_out, "rep").astype(jnp.float32)
    parts, keep = arrange(grads_small)
    cols = half + 2 * state
    where = {h: (k, j) for k in range(2) for j, h in enumerate(lists[k])}

    def ordered(pair, size):
        pieces = []
        for a, b in runs(range(heads)):
            for h in range(a, b):
                k, j = where[h]
                pieces.append(pair[k][..., j * size:(j + 1) * size])
        return jnp.concatenate(pieces, -1)

    col_parts = [v[:8 * cols].reshape(8, cols) for v in parts]
    head_parts = [v[8 * cols:8 * cols + 256].reshape(2, 128) for v in parts]
    col_x = ordered(col_parts, HW)
    col_bc = col_parts[0][:5, half:] + col_parts[1][:5, half:]
    conv_grads = jnp.concatenate([col_x[:5], col_bc], 1)
    head_grads = ordered(head_parts, 1)

    def own(value, axis=-1):
        size = value.shape[axis] // shards
        return lax.dynamic_slice_in_dim(value, shard * size, size, axis % value.ndim)

    return (
        pick(x, jnp.stack(outputs[0]), jnp.stack(outputs[1]))[None],
        pick(x, jnp.stack(in_grads[0]), jnp.stack(in_grads[1]))[None],
        grad_in[None],
        grad_out[None],
        own(conv_grads[:4]).T[None],
        own(conv_grads[4])[None],
        own(head_grads[0])[None],
        own(head_grads[1])[None],
        own(jnp.sum(col_x[6].reshape(heads, HW), -1))[None],
        own(keep[8 * cols + 256:])[None],
        own(col_x[5])[None],
    )


def solution(mesh):
    rows = P(("fsdp", "rep"), None, None)
    return jax.shard_map(
        per_device,
        mesh=mesh,
        in_specs=(rows, rows, P(("fsdp", "rep"), None), P("section", "fsdp", None),
                  P("section", "fsdp", None), P("section", "fsdp", None)) + (P("section", "fsdp"),) * 6,
        out_specs=(P("section", ("fsdp", "rep"), None, None),) * 2
        + (P("section", "fsdp", None),) * 3 + (P("section", "fsdp"),) * 6,
        check_vma=False,
    )
```
